256 devices in a mesh: section: 32 (over x_lo, z, core), expert: 8 (over x_hi, y).
Axes of the slice: x: 4 (x_hi: 2, x_lo: 2; x = x_hi * 2 + x_lo), y: 4, z: 8, core: 2. Of those that a mesh axis runs over, the one named last changes fastest.
Arguments:
- tokens: bfloat16 [2048, 3072], P(('section', 'expert')), may hold values from -6 to 6
- upstream: bfloat16 [2048, 3072], P(('section', 'expert')), may hold values from -2 to 2
- route_ids: int32 [2048, 2], P(('section', 'expert')), may hold values from 0 to 7, all different within a row; in each aligned block of 8 rows (0 to 7, 8 to 15, ...) at most 4 rows name the same one
- route_gates: bfloat16 [2048, 2], P(('section', 'expert')), may hold values from 0.099609375 to 0.8984375
- w_gate: bfloat16 [8, 3072, 8192], P('expert', None, 'section'), may hold values from -0.109375 to 0.109375
- w_up: bfloat16 [8, 3072, 8192], P('expert', None, 'section'), may hold values from -0.109375 to 0.109375
- w_down: bfloat16 [8, 8192, 3072], P('expert', 'section'), may hold values from -0.0625 to 0.0625
Outputs:
- grad_tokens: bfloat16 [2048, 3072], P(('section', 'expert'))
- grad_gates: float32 [2048, 2], P(('section', 'expert'))
- grad_w_gate: bfloat16 [8, 3072, 8192], P('expert', None, 'section')
- grad_w_up: bfloat16 [8, 3072, 8192], P('expert', None, 'section')
- grad_w_down: bfloat16 [8, 8192, 3072], P('expert', 'section')
The draws below stay inside these ranges and needn't reach their ends.
Inputs may be any that keep to these rules, and one draw needn't show every extreme that they name: `route_ids`: the two experts of a token differ. Among the 16 choices of the tokens of one device, each expert is named at most 4 times, and in some device's tokens some expert is named exactly 4 times.
All inputs are finite; a program needn't handle non-finite values.
Results may differ from the reference program's by a relative error of at most 0.0058.
Values may be sent and summed in bfloat16 or wider, within the bound.
A program may use at most 128 MiB of HBM per device.

```python
import math
import jax
import jax.numpy as jnp
import numpy as np
from jax import lax

D = 3072
TOK_DEV = 8
EXPERTS = 8
CAP = 4
F = 8192
TOKENS = 2048


def level_of(rng, dims, split, low, top_value):
    loudness, own = 1.0, jax.random.fold_in(rng, 6)
    for dim, parts in split:
        draws = jnp.exp(jax.random.uniform(jax.random.fold_in(own, dim), (parts,), jnp.float32, low / len(split), top_value / len(split)))
        loudness = loudness * jnp.repeat(draws, dims[dim] // parts).reshape([-1 if axis == dim else 1 for axis in range(len(dims))])
    return loudness


def shared_out(own_key, own, number, rows, count, top, reach, lean):
    sequence = jax.random.permutation(own_key, count)
    heavy_load, usual = portions_of(count, rows * top, reach, lean, True), portions_of(count, rows * top, reach, lean, False)
    places = jnp.arange(count)

    def named(tallies, turn):
        used = int((tallies > 0).sum())
        fixed = max(1, used // 4)
        shifted = fixed + (places - fixed + turn * (used - fixed)) % max(1, count - fixed)
        return jnp.zeros((count,), jnp.int32).at[sequence[jnp.where(places < fixed, places, shifted)]].set(jnp.asarray(tallies, jnp.int32))

    tallies = jnp.where(number % 4 == 0, named(heavy_load, number // 4), named(usual, number - number // 4 - 1))
    mixed = jax.random.permutation(jax.random.fold_in(own, 3), count)
    source_of, receiver = mixed[0:count // 2 * 2:2], mixed[1:count // 2 * 2:2]
    slack = jnp.minimum(tallies[source_of] - 1, reach - tallies[receiver]) // 2
    slack = jnp.where((source_of == sequence[0]) | (receiver == sequence[0]) | (tallies[receiver] == 0), 0, jnp.maximum(slack, 0))
    shifted = jax.random.randint(jax.random.fold_in(own, 4), (count // 2,), 0, 1 << 20) % (slack + 1)
    tallies = tallies.at[source_of].add(-shifted).at[receiver].add(shifted)
    items = jnp.searchsorted(jnp.cumsum(tallies), jnp.arange(rows * top), side="right").astype(jnp.int32)
    table = items.reshape(top, rows).T
    table = table[jax.random.permutation(jax.random.fold_in(own, 1), rows)]
    turn = jax.random.randint(jax.random.fold_in(own, 2), (rows, 1), 0, top)
    return jnp.take_along_axis(table, (jnp.arange(top)[None, :] + turn) % top, axis=1)


def portions_of(number_of, total, reach, lean, full):
    portions = [(1 << 20) // math.isqrt(standing ** lean) + 1 for standing in range(1, number_of + 1)]
    largest = reach if full else min(reach, max(-(-total // number_of), total * portions[0] // sum(portions)))
    least = 1 if total - largest >= number_of - 1 else 0
    holding, spare = [largest] + [least] * (number_of - 1), total - largest - least * (number_of - 1)
    while spare > 0:
        free = [i for i in range(1, number_of) if holding[i] < largest] or [i for i in range(1, number_of) if holding[i] < reach]
        whole, left = sum([portions[i] for i in free]), spare
        for i in free:
            addition = min(reach - holding[i], max(1, left * portions[i] // whole), spare)
            holding[i] = holding[i] + addition
            spare = spare - addition
    return np.array(holding)


def bell_draw(own_key, shape, deviation, reach, pieces=(), kind=jnp.bfloat16):
    entries = deviation * jax.random.normal(own_key, shape, jnp.float32)
    if pieces:
        entries = entries * level_of(own_key, shape, pieces, -0.22, 0.18)
    return jnp.clip(entries, -reach, reach).astype(kind)


def setup_inputs(seed: int = 0) -> dict:
    seeds = jax.random.split(jax.random.key(seed), 8)
    tokens = bell_draw(seeds[0], (TOKENS, D), 1.0, 6.0, ((0, 256),))
    upstream = bell_draw(seeds[1], (TOKENS, D), 0.3, 2.0, ((0, 256),))
    route_ids_keys = jax.random.split(jax.random.fold_in(seeds[2], 1), TOKENS // TOK_DEV)
    route_ids_turns = jax.random.permutation(jax.random.fold_in(seeds[2], 3), TOKENS // TOK_DEV)
    route_ids = jax.vmap(lambda own, number: shared_out(jax.random.fold_in(seeds[2], 2), own, number, TOK_DEV, EXPERTS, 2, CAP, 2))(route_ids_keys, route_ids_turns).reshape((TOKENS, 2))
    route_gates = jnp.clip(0.099609375 + 0.7988281 * jax.random.uniform(seeds[3], (TOKENS, 2), jnp.float32) ** level_of(seeds[3], (TOKENS, 2), ((0, 256),), -0.2, 0.2), 0.099609375, 0.8984375).astype(jnp.bfloat16)
    w_gate = bell_draw(seeds[4], (EXPERTS, D, F), D ** -0.5, 0.109375, ((0, 8), (2, 32)))
    w_up = bell_draw(seeds[5], (EXPERTS, D, F), D ** -0.5, 0.109375, ((0, 8), (2, 32)))
    w_down = bell_draw(seeds[6], (EXPERTS, F, D), F ** -0.5, 0.0625, ((0, 8), (1, 32)))
    return dict(tokens=tokens, upstream=upstream, route_ids=route_ids, route_gates=route_gates, w_gate=w_gate, w_up=w_up, w_down=w_down)


def one_expert(operands):
    rows_x, rows_dy, rows_weight, gate_slab, up_slab, down_slab = operands
    pre_gate = jnp.dot(rows_x, gate_slab, preferred_element_type=jnp.float32)
    pre_up = jnp.dot(rows_x, up_slab, preferred_element_type=jnp.float32)
    sigmoid_gate = jax.nn.sigmoid(pre_gate)
    active = pre_gate * sigmoid_gate
    hidden = (active * pre_up).astype(jnp.bfloat16)
    expert_out = jnp.dot(hidden, down_slab, preferred_element_type=jnp.float32)
    gate_grad = jnp.sum(rows_dy.astype(jnp.float32) * expert_out, axis=1)
    back_proj = jnp.dot(rows_dy, down_slab.T, preferred_element_type=jnp.float32)
    weight = rows_weight[:, None]
    d_hidden = weight * back_proj
    d_gate = (d_hidden * pre_up * (sigmoid_gate * (1.0 + pre_gate * (1.0 - sigmoid_gate)))).astype(jnp.bfloat16)
    d_up = (d_hidden * active).astype(jnp.bfloat16)
    scaled_up = (weight * rows_dy.astype(jnp.float32)).astype(jnp.bfloat16)
    grad_down = jnp.dot(hidden.T, scaled_up, preferred_element_type=jnp.float32).astype(jnp.bfloat16)
    grad_gate = jnp.dot(rows_x.T, d_gate, preferred_element_type=jnp.float32).astype(jnp.bfloat16)
    grad_up = jnp.dot(rows_x.T, d_up, preferred_element_type=jnp.float32).astype(jnp.bfloat16)
    grad_rows = jnp.dot(d_gate, gate_slab.T, preferred_element_type=jnp.float32) + jnp.dot(d_up, up_slab.T, preferred_element_type=jnp.float32)
    return grad_rows, gate_grad, grad_gate, grad_up, grad_down


def reference(tokens, upstream, route_ids, route_gates, w_gate, w_up, w_down):
    blocks = TOKENS // TOK_DEV
    flattened = route_ids.reshape(blocks, 2 * TOK_DEV).astype(jnp.int32)
    onehot = (flattened[:, :, None] == jnp.arange(EXPERTS, dtype=jnp.int32)[None, None, :]).astype(jnp.int32)
    before = jnp.cumsum(onehot, axis=1) - onehot
    position = jnp.sum(before * onehot, axis=2).astype(jnp.int32)
    block_ids = jnp.arange(blocks, dtype=jnp.int32)[:, None]
    target = (flattened * (blocks * CAP) + block_ids * CAP + position).reshape(-1).astype(jnp.int32)
    slot_total = EXPERTS * blocks * CAP
    tokens_twice = jnp.repeat(tokens, 2, axis=0)
    upstream_twice = jnp.repeat(upstream, 2, axis=0)
    gates_flat = route_gates.reshape(-1).astype(jnp.float32)
    buffer_x = jnp.zeros((slot_total, D), jnp.bfloat16).at[target].set(tokens_twice).reshape(EXPERTS, blocks * CAP, D)
    buffer_dy = jnp.zeros((slot_total, D), jnp.bfloat16).at[target].set(upstream_twice).reshape(EXPERTS, blocks * CAP, D)
    buffer_weight = jnp.zeros((slot_total,), jnp.float32).at[target].set(gates_flat).reshape(EXPERTS, blocks * CAP)
    grad_rows, gate_grad, grad_gate, grad_up, grad_down = lax.map(one_expert, (buffer_x, buffer_dy, buffer_weight, w_gate, w_up, w_down))
    row_grads = grad_rows.reshape(slot_total, D)[target]
    grad_tokens = jnp.sum(row_grads.reshape(TOKENS, 2, D), axis=1).astype(jnp.bfloat16)
    grad_gates = gate_grad.reshape(slot_total)[target].reshape(TOKENS, 2)
    return grad_tokens, grad_gates, grad_gate, grad_up, grad_down
```

```python
import jax
import jax.numpy as jnp
from jax import lax
from jax.sharding import PartitionSpec as P


def slot_matrix(route_ids, experts, capacity):
    flattened = route_ids.reshape(-1)
    onehot = (flattened[:, None] == jnp.arange(experts, dtype=jnp.int32)[None, :]).astype(jnp.int32)
    before = jnp.cumsum(onehot, axis=0) - onehot
    position = jnp.sum(before * onehot, axis=1)
    target = flattened * capacity + position
    columns = jnp.arange(experts * capacity, dtype=jnp.int32)
    return target[:, None] == columns[None, :]


def contract_last(left, right):
    return lax.dot_general(
        left, right, (((1,), (1,)), ((), ())), preferred_element_type=jnp.float32
    )


def contract_first(left, right):
    return lax.dot_general(
        left, right, (((0,), (0,)), ((), ())), preferred_element_type=jnp.float32
    )


def local(tokens, upstream, route_ids, route_gates, w_gate, w_up, w_down):
    experts = lax.axis_size("expert")
    tok_count, features = tokens.shape
    capacity = min(tok_count, max(2, 4 * tok_count // experts))
    chosen_slots = slot_matrix(route_ids, experts, capacity)
    placement = chosen_slots.astype(jnp.bfloat16)
    gates = route_gates.reshape(-1).astype(jnp.float32)
    tokens_twice = jnp.repeat(tokens, 2, axis=0)
    scaled = (gates[:, None] * jnp.repeat(upstream, 2, axis=0).astype(jnp.float32)).astype(
        jnp.bfloat16
    )
    send_x = contract_first(placement, tokens_twice).astype(jnp.bfloat16)
    send_u = contract_first(placement, scaled).astype(jnp.bfloat16)
    send = jnp.concatenate(
        [send_x.reshape(experts, capacity, features), send_u.reshape(experts, capacity, features)],
        axis=1,
    )
    recv = lax.all_to_all(send, "expert", split_axis=0, concat_axis=0, tiled=True)
    mine = jnp.stack([recv[:, :capacity], recv[:, capacity:]]).reshape(
        2, experts * capacity, features
    )
    every = lax.all_gather(mine, "section", axis=1, tiled=True)
    rows_x, rows_u = every[0], every[1]
    gate_slab = w_gate[0]
    up_slab = w_up[0]
    down_slab = w_down[0]
    pre_gate = jnp.dot(rows_x, gate_slab, preferred_element_type=jnp.float32)
    pre_up = jnp.dot(rows_x, up_slab, preferred_element_type=jnp.float32)
    sigmoid_gate = jax.nn.sigmoid(pre_gate)
    active = pre_gate * sigmoid_gate
    hidden = (active * pre_up).astype(jnp.bfloat16)
    d_hidden = contract_last(rows_u, down_slab)
    d_gate = (d_hidden * pre_up * (sigmoid_gate * (1.0 + pre_gate * (1.0 - sigmoid_gate)))).astype(
        jnp.bfloat16
    )
    d_up = (d_hidden * active).astype(jnp.bfloat16)
    grad_down = contract_first(hidden, rows_u)
    grad_gate = contract_first(rows_x, d_gate)
    grad_up = contract_first(rows_x, d_up)
    input_part = contract_last(d_gate, gate_slab) + contract_last(d_up, up_slab)
    gate_part = hidden.astype(jnp.float32) * d_hidden
    units = gate_part.shape[1]
    gate_part = sum(gate_part[:, i : i + 128] for i in range(0, units, 128))
    part = jnp.concatenate([input_part, gate_part], axis=1)
    part_mine = lax.psum_scatter(part, "section", scatter_dimension=0, tiled=True)
    back = lax.all_to_all(
        part_mine.reshape(experts, capacity, features + 128),
        "expert",
        split_axis=0,
        concat_axis=0,
        tiled=True,
    ).reshape(experts * capacity, features + 128)
    selector = chosen_slots.astype(jnp.float32)
    choice = jnp.dot(selector, back, precision=lax.Precision.HIGHEST)
    grad_tokens = jnp.sum(choice[:, :features].reshape(tok_count, 2, features), axis=1)
    grad_gates = (jnp.sum(choice[:, features:], axis=1) / gates).reshape(tok_count, 2)
    return (
        grad_tokens.astype(jnp.bfloat16),
        grad_gates,
        grad_gate.astype(jnp.bfloat16)[None],
        grad_up.astype(jnp.bfloat16)[None],
        grad_down.astype(jnp.bfloat16)[None],
    )


def solution(mesh):
    placed = (
        P(("section", "expert"), None),
        P(("section", "expert"), None),
        P(("section", "expert"), None),
        P(("section", "expert"), None),
        P("expert", None, "section"),
        P("expert", None, "section"),
        P("expert", "section", None),
    )
    return jax.shard_map(
        local,
        mesh=mesh,
        in_specs=placed,
        out_specs=(
            P(("section", "expert"), None),
            P(("section", "expert"), None),
            P("expert", None, "section"),
            P("expert", None, "section"),
            P("expert", "section", None),
        ),
        check_vma=False,
    )
```
